32 devices in a mesh: seq: 4 (over y, x), dp: 2 (over core), mp: 4 (over z).
Axes of the slice: x: 2, y: 2, z: 4, core: 2. Of those that a mesh axis runs over, the one named last changes fastest.
Arguments:
- tokens: bfloat16 [8, 2048, 2048], P('dp', 'seq', 'mp'), may hold values from -6 to 6
- cotangent: bfloat16 [8, 2048, 2048], P('dp', 'seq', 'mp'), may hold values from -6 to 6
- domain_id: int32 [8], P('dp'), may hold values from 0 to 7
- domain_weight: int32 [8], replicated, may hold values from 1 to 4
- lower_level: int32 [2048], P('mp'), may hold values from 2 to 23
- norm_in: float32 [2048], P('mp'), may hold values from 0.1 to 1.9
- w_input: bfloat16 [2048, 2048], P(None, 'mp'), may hold values from -0.125 to 0.125
- w_forget: bfloat16 [2048, 2048], P(None, 'mp'), may hold values from -0.125 to 0.125
- w_gate_out: bfloat16 [2048, 2048], P(None, 'mp'), may hold values from -0.125 to 0.125
- out_gain: float32 [2048], P('mp'), may hold values from 0.1 to 1.9
- w_out: bfloat16 [2048, 2048], P('mp'), may hold values from -0.125 to 0.125
- norm_mid: float32 [2048], P('mp'), may hold values from 0.1 to 1.9
- w_gate: bfloat16 [2048, 5632], P(None, 'mp'), may hold values from -0.125 to 0.125
- w_up: bfloat16 [2048, 5632], P(None, 'mp'), may hold values from -0.125 to 0.125
- w_down: bfloat16 [5632, 2048], P('mp'), may hold values from -0.078125 to 0.078125
Outputs:
- mixed: bfloat16 [8, 2048, 2048], P('dp', 'seq', 'mp')
- grad_tokens: float32 [8, 2048, 2048], P('dp', 'seq', 'mp')
- grad_norm_in: float32 [2048], P('mp')
- grad_w_input: float32 [2048, 2048], P(None, 'mp')
- grad_w_forget: float32 [2048, 2048], P(None, 'mp')
- grad_w_gate_out: float32 [2048, 2048], P(None, 'mp')
- grad_out_gain: float32 [2048], P('mp')
- grad_w_out: float32 [2048, 2048], P('mp')
- grad_norm_mid: float32 [2048], P('mp')
- grad_w_gate: float32 [2048, 5632], P(None, 'mp')
- grad_w_up: float32 [2048, 5632], P(None, 'mp')
- grad_w_down: float32 [5632, 2048], P('mp')
The draws below stay inside these ranges and needn't reach their ends.
All inputs are finite; a program needn't handle non-finite values.
Results may differ from the reference program's by a relative error of at most 0.0075.
The reference program's roundings to bfloat16 on the way count: a program that leaves them out, or rounds other values in their place, can miss the bound.
Values may be sent and summed in bfloat16 or wider, within the bound.
No kernel may reach another device: no remote copies, remote signals or barrier semaphores. Data moves between devices by JAX's collectives and lax.ppermute only.
A program may use at most 320 MiB of HBM per device.

```python
import jax
import jax.numpy as jnp
from jax import lax

D = 2048
FF = 5632
LEN = 2048
DOMAINS = 8
NSEQ = 8


def place_ends(entries, key, smallest, largest):
    shape = entries.shape
    spot = [jax.random.randint(jax.random.fold_in(key, axis), (), 0, shape[axis]) for axis in range(len(shape))]
    entries = entries.at[tuple(spot)].set(smallest)
    longest = shape.index(max(shape))
    spot[longest] = (spot[longest] + 1) % shape[longest]
    return entries.at[tuple(spot)].set(largest)


def steps_of(stream_key, shape, shards, smallest, high):
    def one(position, parts):
        steps = jax.random.uniform(jax.random.fold_in(jax.random.fold_in(stream_key, 6), position), (parts,), jnp.float32, smallest / len(shards), high / len(shards))
        return jnp.repeat(jnp.exp(steps), shape[position] // parts).reshape((-1,) + (1,) * (len(shape) - position - 1))

    level = one(*shards[0])
    for cut in shards[1:]:
        level = level * one(*cut)
    return level


def normal_values(stream_key, dims, deviation, bound, split=(), held_as=jnp.bfloat16):
    result = jax.random.normal(stream_key, dims, jnp.float32) * deviation
    if len(split) > 0:
        result = steps_of(stream_key, dims, split, -0.22, 0.18) * result
    return jnp.clip(result, min=-bound, max=bound).astype(held_as)


def setup_inputs(seed: int = 0) -> dict:
    seeds = jax.random.split(jax.random.key(seed), 16)
    return {
        "tokens": normal_values(seeds[0], (NSEQ, LEN, D), 1.0, 6.0, ((0, 2), (1, 4), (2, 4))),
        "cotangent": normal_values(seeds[1], (NSEQ, LEN, D), 1.0, 6.0, ((0, 2), (1, 4), (2, 4))),
        "domain_id": place_ends(jax.random.randint(seeds[2], (NSEQ,), 0, DOMAINS), jax.random.fold_in(seeds[2], 1), 0, DOMAINS - 1).astype(jnp.int32),
        "domain_weight": place_ends(jax.random.randint(seeds[3], (DOMAINS,), 1, 5), jax.random.fold_in(seeds[3], 1), 1, 4).astype(jnp.int32),
        "lower_level": place_ends(jax.random.randint(seeds[4], (D,), 2, 24), jax.random.fold_in(seeds[4], 1), 2, 23).astype(jnp.int32),
        "norm_in": jnp.clip(1.0 + 0.18 * jax.random.normal(seeds[5], (D,), jnp.float32), 0.1, 1.9),
        "w_input": normal_values(seeds[6], (D, D), D ** -0.5, 0.125, ((1, 4),)),
        "w_forget": normal_values(seeds[7], (D, D), D ** -0.5, 0.125, ((1, 4),)),
        "w_gate_out": normal_values(seeds[8], (D, D), D ** -0.5, 0.125, ((1, 4),)),
        "out_gain": jnp.clip(1.0 + 0.18 * jax.random.normal(seeds[9], (D,), jnp.float32), 0.1, 1.9),
        "w_out": normal_values(seeds[10], (D, D), D ** -0.5, 0.125, ((0, 4),)),
        "norm_mid": jnp.clip(1.0 + 0.18 * jax.random.normal(seeds[11], (D,), jnp.float32), 0.1, 1.9),
        "w_gate": normal_values(seeds[12], (D, FF), D ** -0.5, 0.125, ((1, 4),)),
        "w_up": normal_values(seeds[13], (D, FF), D ** -0.5, 0.125, ((1, 4),)),
        "w_down": normal_values(seeds[14], (FF, D), FF ** -0.5, 0.078125, ((0, 4),)),
    }


EPS = 1e-06

@jax.custom_vjp
def low(v):
    return lax.optimization_barrier(v.astype(jnp.bfloat16)).astype(jnp.float32)

@jax.custom_vjp
def low_back(v):
    return v

def low_keep(v):
    return (low(v), None)

def low_pass(kept, grad):
    return (grad,)

def back_keep(v):
    return (v, None)

def back_low(kept, grad):
    return (low(grad),)
low.defvjp(low_keep, low_pass)
low_back.defvjp(back_keep, back_low)

def matmul(left, right):
    return jnp.dot(left, right, precision=lax.Precision.HIGHEST, preferred_element_type=jnp.float32)

def rms_scale(values):
    return lax.rsqrt(lax.optimization_barrier(jnp.mean(values * values, axis=-1, keepdims=True)) + EPS)

def chain_pairs(earlier, later):
    return (earlier[0] * later[0], later[0] * earlier[1] + later[1])

def block(inputs, params, lower):
    norm_in, w_input, w_forget, w_gate_out, out_gain, w_out, norm_mid, w_gate, w_up, w_down = params
    normed = low(inputs * rms_scale(inputs) * norm_in)
    in_raw = low_back(matmul(normed, w_input))
    forget_raw = low_back(matmul(normed, w_forget))
    gate_raw = low_back(matmul(normed, w_gate_out))
    forget = lower + (1.0 - lower) * jax.nn.sigmoid(forget_raw)
    inflow = jax.nn.silu(in_raw) * (1.0 - forget)
    decay_run, state = lax.associative_scan(chain_pairs, (forget, inflow), axis=0)
    gated = low(state * rms_scale(state) * out_gain * jax.nn.silu(gate_raw))
    resid = inputs + low_back(matmul(gated, w_out))
    second = low(resid * rms_scale(resid) * norm_mid)
    gate_value = low_back(matmul(second, w_gate))
    up_value = low_back(matmul(second, w_up))
    hidden_act = low(jax.nn.silu(gate_value) * up_value)
    return resid + low_back(matmul(hidden_act, w_down))

def reference(tokens, cotangent, domain_id, domain_weight, lower_level, norm_in, w_input, w_forget, w_gate_out, out_gain, w_out, norm_mid, w_gate, w_up, w_down):
    params = tuple((item.astype(jnp.float32) for item in (norm_in, w_input, w_forget, w_gate_out, out_gain, w_out, norm_mid, w_gate, w_up, w_down)))
    lower = 1.0 - jnp.exp2(-0.5 * lower_level.astype(jnp.float32))
    seq_weight = domain_weight[domain_id].astype(jnp.float32)

    def run_block(inputs, weights):
        return block(inputs, weights, lower)

    def one_sequence(grads, item):
        inputs, grad_in, weight = item
        block_out, pullback = jax.vjp(run_block, inputs.astype(jnp.float32), params)
        grad_inputs, grad_params = pullback(grad_in.astype(jnp.float32) * weight)
        summed = tuple((total + part for total, part in zip(grads, grad_params)))
        return (summed, (block_out.astype(jnp.bfloat16), grad_inputs))
    start = tuple((jnp.zeros_like(item) for item in params))
    grads, outputs = lax.scan(one_sequence, start, (tokens, cotangent, seq_weight))
    return (outputs[0], outputs[1], grads[0], grads[1], grads[2], grads[3], grads[4], grads[5], grads[6], grads[7], grads[8], grads[9])
```

```python
import jax
import jax.numpy as jnp
from jax import lax
from jax.experimental import pallas as pl
from jax.experimental.pallas import tpu as pltpu
from jax.sharding import PartitionSpec as P

EPS = 1e-06
F32 = jnp.float32
BF16 = jnp.bfloat16
LANES = 8


def scan_body(backward, a_ref, b_ref, d_ref, e_ref, td_ref, te_ref):
    seqs, count, width = a_ref.shape
    seg = count // LANES

    def step(j, carry):
        at = seg - 1 - j if backward else j
        rows = pl.ds(at, LANES, stride=seg)
        after = []
        for i, (decay, run) in enumerate(carry):
            d_ref[i, rows, :] = decay
            e_ref[i, rows, :] = run
            factor = a_ref[i, rows, :]
            after.append((factor * decay, factor * run + b_ref[i, rows, :]))
        return tuple(after)

    start = (jnp.ones((LANES, width), F32), jnp.zeros((LANES, width), F32))
    ends = lax.fori_loop(0, seg, step, (start,) * seqs, unroll=4)
    for i, (decay, run) in enumerate(ends):
        carry_d = jnp.ones((1, width), F32)
        carry_e = jnp.zeros((1, width), F32)
        for g in reversed(range(LANES)) if backward else range(LANES):
            rows = pl.ds(g * seg, seg)
            inner = d_ref[i, rows, :]
            e_ref[i, rows, :] = e_ref[i, rows, :] + inner * carry_e
            d_ref[i, rows, :] = inner * carry_d
            own_d, own_e = (decay[g : g + 1, :], run[g : g + 1, :])
            carry_d, carry_e = (carry_d * own_d, own_d * carry_e + own_e)
        td_ref[i] = carry_d
        te_ref[i] = carry_e


def linear_scan(factor, term, backward):
    seqs, count, width = factor.shape
    lanes = 128
    block = pl.BlockSpec((seqs, count, lanes), lambda i: (0, 0, i))
    last = pl.BlockSpec((seqs, 1, lanes), lambda i: (0, 0, i))
    whole = jax.ShapeDtypeStruct(factor.shape, F32)
    total = jax.ShapeDtypeStruct((seqs, 1, width), F32)
    return pl.pallas_call(
        lambda *refs: scan_body(backward, *refs),
        grid=(width // lanes,),
        in_specs=[block, block],
        out_specs=[block, block, last, last],
        out_shape=[whole, whole, total, total],
        name="scan_back" if backward else "scan_fwd",
    )(factor, term)


def dot(left, right):
    return jnp.dot(left, right, preferred_element_type=F32)


def dot_t(left, right):
    return lax.dot_general(left, right, (((1,), (1,)), ((), ())), preferred_element_type=F32)


def t_dot(left, right):
    return lax.dot_general(left, right, (((0,), (0,)), ((), ())), preferred_element_type=F32)


def sigmoid(v):
    return jax.nn.sigmoid(v)


def after(value, *earlier):
    return lax.optimization_barrier((value, earlier))[0]


def bits_of(count):
    return [1 << i for i in range(count.bit_length() - 1)]


def per_device(
    tokens,
    cotangent,
    domain_id,
    domain_weight,
    lower_level,
    norm_in,
    w_input,
    w_forget,
    w_gate_out,
    out_gain,
    w_out,
    norm_mid,
    w_gate,
    w_up,
    w_down,
):
    n_seq, n_core, n_mp = (lax.axis_size(axis) for axis in ("seq", "dp", "mp"))
    assert n_core == 2
    half = n_mp // 2
    group = n_mp
    seqs, length, width = tokens.shape
    rows = seqs * length
    chunk = rows // group
    full = width * n_mp
    block = full // n_seq
    ff = w_gate.shape[1]
    s, c, m = (lax.axis_index(axis) for axis in ("seq", "dp", "mp"))
    part, low = (m // half, m % half)
    q = low + half * (part ^ c)
    v = low + half * c

    group_bits = bits_of(half) + [half]

    def hop(value, bit):
        if bit == half:
            return lax.ppermute(value, "dp", [(0, 1), (1, 0)])
        return lax.ppermute(value, "mp", [(i, i ^ bit) for i in range(n_mp)])

    def gather_group(value):
        pieces = {0: value}
        for bit in group_bits:
            for k in list(pieces):
                pieces[k | bit] = hop(pieces[k], bit)
        return [pieces[k] for k in range(group)]

    remote_first = sorted(range(group), key=lambda k: (-(k % half), k // half == 0))

    def scatter_group(partial, holds, fill):
        live = dict(partial)
        for bit in reversed(group_bits):
            for k in [k for k in remote_first if k in live and k & bit]:
                sent = live.pop(k).astype(BF16)
                if len(live) == 1:
                    holds = fill(sent) if callable(fill) else fill
                received = after(hop(sent, bit), holds)
                live[k ^ bit] = live[k ^ bit] + received.astype(F32)
        return live[0], sent

    def sum_group(value, fill=()):
        for bit in group_bits:
            value = value + after(hop(value, bit), fill if bit == half else ())
        return value

    def place(core, at):
        return core * n_mp + at

    crossing = [
        (place(core, at), place(1 - core, at ^ half))
        for core in range(2)
        for at in range(n_mp)
        if at // half != core
    ]

    def to_native(value, fill=()):
        got = after(lax.ppermute(value, ("dp", "mp"), crossing), fill)
        return jnp.where(c == part, value, got)

    seq_bits = len(bits_of(n_seq))
    straight = list(range(seq_bits))
    crossed = straight[::-1]

    def rows_of(value, at, count):
        return lax.dynamic_slice_in_dim(value, at * count, count, 0)

    def cols_of(value, at, count):
        return lax.dynamic_slice_in_dim(value, at * count, count, 1)

    def join(parts, spot, count, shape, axis, dtype):
        total = jnp.zeros(shape, dtype)
        for k, value in enumerate(parts):
            total = lax.dynamic_update_slice_in_dim(total, value, spot(k) * count, axis)
        return total

    def fetch_start(*own):
        count = own[0].shape[0] // (2 * n_seq)
        pieces = [rows_of(value, s * 2 + c, count) for value in own]
        return lax.ppermute(jnp.concatenate(pieces, 1), "mp", [(i, i ^ half) for i in range(n_mp)])

    def fetch_end(piece, *own):
        there = lax.all_gather(piece, ("seq", "dp"), axis=0, tiled=True)
        whole, at = ([], 0)
        for value in own:
            wide = value.shape[1]
            whole.append(jnp.where(c == 1, there[:, at : at + wide], value))
            at += wide
        return whole

    def total_of(left, right):
        return (left.astype(F32) + right.astype(F32)).astype(BF16)

    def sync(value, order, gates):
        height, wide = value.shape
        value = value.reshape((2,) * seq_bits + (height // n_seq, wide))
        left = crossed.copy()
        for bit, gate in zip(order, gates, strict=True):
            axis = left.index(bit)
            here = (s >> bit) & 1
            away = lax.dynamic_index_in_dim(value, 1 - here, axis, keepdims=False)
            kept = lax.dynamic_index_in_dim(value, here, axis, keepdims=False)
            away = lax.ppermute(away, "seq", [(i, i ^ (1 << bit)) for i in range(n_seq)])
            value = total_of(kept, after(away, gate))
            left.remove(bit)
        return value

    def combine(value, gate, gate_core):
        other = lax.ppermute(
            value, ("dp", "mp"), [(place(1, i), place(0, i ^ half)) for i in range(n_mp)]
        )
        value = total_of(value, after(other, gate))
        cut = value.shape[0] // 2
        lower_part = after(lax.ppermute(value[cut:], "dp", [(0, 1)]), gate_core)
        return jnp.where(c == 0, value[:cut], lower_part)

    def spread(value):
        return lax.all_gather(value, ("seq", "dp"), axis=0, tiled=True)

    small = jnp.stack((norm_in, norm_mid, out_gain, lower_level.astype(F32)))
    small = small[None]
    for bit in bits_of(n_mp):
        there = lax.ppermute(small, "mp", [(i, i ^ bit) for i in range(n_mp)])
        small = jnp.concatenate((small, there), 0)

    def small_of(at, row):
        return lax.dynamic_index_in_dim(small[:, row], m ^ at, 0, keepdims=False)

    gain_mid = jnp.concatenate([small_of(k, 1) for k in range(n_mp)])
    gain_out = small_of(q, 2)
    lower_level = small_of(q, 3)
    lower = 1.0 - jnp.exp2(-0.5 * lower_level)
    domain_hits = domain_id[:, None] == jnp.arange(domain_weight.shape[0], dtype=jnp.int32)[None, :]
    seq_weight = jnp.sum(jnp.where(domain_hits, domain_weight[None, :], 0), 1).astype(F32)
    seq_weight = jnp.where(c == part, seq_weight, lax.ppermute(seq_weight, "dp", [(0, 1), (1, 0)]))
    row_weight = jnp.broadcast_to(seq_weight[:, None], (seqs, length)).reshape(rows, 1)

    mix_piece = fetch_start(w_input, w_forget, w_gate_out)
    x_own = to_native(tokens.reshape(rows, width))
    mix_piece, x_own = lax.optimization_barrier((mix_piece, x_own))
    x_parts = gather_group(x_own)
    w_in, w_fg, w_go = fetch_end(mix_piece, w_input, w_forget, w_gate_out)
    out_piece = fetch_start(after(w_out, x_own))
    pair_piece = fetch_start(*after((w_gate, w_up), x_own))
    out_piece, pair_piece, x_parts[1] = lax.optimization_barrier((out_piece, pair_piece, x_parts[1]))
    x_parts[1] = after(x_parts[1], w_in, w_fg, w_go)
    (out_w,) = fetch_end(out_piece, w_out)
    gate_w, up_w = fetch_end(pair_piece, w_gate, w_up)
    squares = sum(jnp.sum(jnp.square(part_x.astype(F32)), 1) for part_x in x_parts)
    scale_in = lax.rsqrt(squares / full + EPS)[:, None]
    normed = join(
        [
            (
                part_x.astype(F32)
                * scale_in
                * small_of(v ^ k, 0)
            ).astype(BF16)
            for k, part_x in enumerate(x_parts)
        ],
        lambda k: v ^ k,
        width,
        (rows, full),
        1,
        BF16,
    )
    x_chunk = join(
        [rows_of(part_x, q, chunk) for part_x in x_parts],
        lambda k: v ^ k,
        width,
        (chunk, full),
        1,
        BF16,
    ).astype(F32)

    in_raw = dot(normed, w_in)
    forget_raw = dot(normed, w_fg)
    forget_sig = sigmoid(forget_raw)
    forget = lower + (1.0 - lower) * forget_sig
    in_sig = sigmoid(in_raw)
    in_act = in_raw * in_sig
    inflow = in_act * (1.0 - forget)
    gate_raw = dot(normed, w_go)
    shape3 = (seqs, length, width)

    def carry(decay, run, backward, fill=()):
        both = jnp.concatenate((decay, run), 1)
        total = jnp.zeros((seqs, width), F32)
        for d in range(n_seq - 1, 0, -1):
            step = -d if backward else d
            pairs = [(i, i + step) for i in range(n_seq) if 0 <= i + step < n_seq]
            got = after(lax.ppermute(both, "seq", pairs), fill)
            total = got[:, 0] * total + got[:, 1]
        return total[:, None, :]

    decay_run, state_run, decay_all, state_all = linear_scan(
        forget.reshape(shape3), inflow.reshape(shape3), False
    )
    state_in = carry(decay_all, state_all, False, (gate_raw,))
    prev = (state_run + decay_run * state_in).reshape(rows, width)
    state = forget * prev + inflow
    scale_state = lax.rsqrt(sum_group(jnp.sum(state * state, 1)) / full + EPS)[:, None]
    state_hat = state * scale_state
    gate_sig = sigmoid(gate_raw)
    gate_act = gate_raw * gate_sig
    gated = (state_hat * gain_out * gate_act).astype(BF16)
    branch_terms = {k: dot(rows_of(gated, q ^ k, chunk), out_w) for k in remote_first}
    branch, branch_sent = scatter_group(branch_terms, (), (branch_terms[0], gate_w, up_w))
    down_piece = fetch_start(after(w_down, branch_sent))
    cot_own = to_native(after(cotangent, branch_sent).reshape(rows, width), (branch,))
    down_piece, branch = lax.optimization_barrier((down_piece, branch))
    (down_w,) = fetch_end(down_piece, w_down)
    resid = x_chunk + branch
    scale_mid = lax.rsqrt(jnp.mean(resid * resid, 1, keepdims=True) + EPS)
    resid_hat = resid * scale_mid
    seconds = gather_group((resid_hat * gain_mid).astype(BF16))
    cot_parts = gather_group(after(cot_own, seconds[half]))

    hids, dzs, d_gates, d_ups, gates, acts = ([None] * group for _ in range(6))
    local_first = sorted(range(group), key=lambda k: (k % half, k))
    for k in local_first:
        local = (hids[0], hids[half]) if k % half else ()
        second = after(seconds[k], local)
        gates[k] = (dot(second, gate_w), dot(second, up_w))
        acts[k] = gates[k][0] * sigmoid(gates[k][0])
        hids[k] = (acts[k] * gates[k][1]).astype(BF16)
    cot_parts = [after(value, hids[0], hids[half]) if k % half else value for k, value in enumerate(cot_parts)]
    cot = join(cot_parts, lambda k: v ^ k, width, (rows, full), 1, BF16)
    d_seconds = {}
    for k in remote_first:
        remote = () if k % half else tuple(d_seconds[j] for j in remote_first if j % half)
        dzs[k] = (
            rows_of(cot, q ^ k, chunk).astype(F32) * rows_of(row_weight, q ^ k, chunk)
        ).astype(BF16)
        d_hid = dot_t(after(dzs[k], remote), down_w)
        gate, up = gates[k]
        sig = sigmoid(gate)
        d_gates[k] = (d_hid * up * (sig * (1.0 + gate * (1.0 - sig)))).astype(BF16)
        d_ups[k] = (d_hid * acts[k]).astype(BF16)
        d_seconds[k] = dot_t(d_gates[k], gate_w) + dot_t(d_ups[k], up_w)
    kept = []

    def fill(sent):
        kept.append(t_dot(jnp.concatenate(after(hids, sent), 0), jnp.concatenate(dzs, 0)).astype(BF16))
        return (kept[0], d_seconds[0])

    d_second, _ = scatter_group(d_seconds, (), fill)
    down_term = kept[0]

    grad_norm_mid = jnp.sum(d_second * resid_hat, 0)
    d_hat = d_second * gain_mid
    mid_dot = jnp.mean(d_hat * resid_hat, 1, keepdims=True)
    d_out = rows_of(cot, q, chunk).astype(F32) * rows_of(row_weight, q, chunk)
    d_resid = d_out + scale_mid * (d_hat - resid_hat * mid_dot)
    d_resids = gather_group(d_resid.astype(BF16))

    second_all = after(jnp.concatenate(seconds, 0), d_resids[0])
    d_pair = jnp.concatenate([jnp.concatenate((d_gates[k], d_ups[k]), 1) for k in range(group)], 0)
    pair_term = t_dot(second_all, d_pair).astype(BF16)
    d_resids = [
        after(value, pair_term) if k % half else value
        for k, value in enumerate(d_resids)
    ]

    def scatter_seq(value):
        return lax.psum_scatter(value, "seq", scatter_dimension=0, tiled=True)

    down_sum, pair_sum = (scatter_seq(value) for value in (down_term, pair_term))

    d_gated = join(
        [dot_t(value, out_w) for value in d_resids],
        lambda k: q ^ k,
        chunk,
        (rows, width),
        0,
        F32,
    )
    outs = {k: dot(after(hids[k], d_gated), down_w) for k in remote_first}
    grad_out_gain = jnp.sum(d_gated * state_hat * gate_act, 0)
    d_gate_raw = (
        d_gated * state_hat * gain_out * (gate_sig * (1.0 + gate_raw * (1.0 - gate_sig)))
    ).astype(BF16)
    d_state_hat = d_gated * gain_out * gate_act
    gate_out_term = t_dot(normed, d_gate_raw).astype(BF16)
    state_dot = sum_group(jnp.sum(d_state_hat * state_hat, 1), (gate_out_term,))[:, None] / full
    d_state = scale_state * (d_state_hat - state_hat * state_dot)
    back_decay, back_run, back_decay_all, back_run_all = linear_scan(
        forget.reshape(shape3), (forget * d_state).reshape(shape3), True
    )
    d_resid_all = jnp.concatenate(d_resids, 0)
    gated_all = jnp.concatenate([rows_of(gated, q ^ k, chunk) for k in range(group)], 0)
    out_term = t_dot(gated_all, d_resid_all).astype(BF16)
    later_in = carry(back_decay_all, back_run_all, True, (out_term,))
    adjoint = d_state + (back_run + back_decay * later_in).reshape(rows, width)
    d_in = (adjoint * (1.0 - forget) * (in_sig * (1.0 + in_raw * (1.0 - in_sig)))).astype(BF16)
    d_forget = (
        (adjoint * prev - adjoint * in_act) * (1.0 - lower) * forget_sig * (1.0 - forget_sig)
    ).astype(BF16)
    down_ready = combine(after(down_sum, d_gated), back_run_all, later_in)
    d_in_here = after(d_in, down_ready)
    d_terms = {
        k: dot_t(d_in_here, rows_of(w_in, v ^ k, width))
        + dot_t(d_forget, rows_of(w_fg, v ^ k, width))
        + dot_t(d_gate_raw, rows_of(w_go, v ^ k, width))
        for k in remote_first
    }
    both_term = t_dot(normed, after(jnp.concatenate((d_in, d_forget), 1), d_terms[1])).astype(BF16)
    in_term, forget_term = (both_term[:, :width], both_term[:, width:])
    pair_ready = combine(after(pair_sum, d_in), d_terms[1], d_terms[0])
    mixed, _ = scatter_group(outs, (state_dot,), (later_in,))
    mixed = (resid + mixed).astype(BF16)
    arrived = {0: cols_of(mixed, v, width)}
    for k in range(1, group):
        pairs = [
            (place(core, at), place(core ^ (k // half), at ^ (k % half)))
            for core in range(2)
            for at in range(n_mp)
        ]
        arrived[k] = after(
            lax.ppermute(cols_of(mixed, v ^ k, width), ("dp", "mp"), pairs), d_terms[1]
        )
    mixed = join(
        [arrived[k] for k in range(group)], lambda k: q ^ k, chunk, (rows, width), 0, BF16
    )
    vectors = jnp.zeros((2, full), F32)
    vectors = lax.dynamic_update_slice(vectors, grad_out_gain[None], (0, q * width))
    vectors = lax.dynamic_update_slice(vectors, grad_norm_mid[None], (1, 0))
    vectors = lax.psum(after(vectors, later_in), ("seq", "dp", "mp"))
    vectors = lax.dynamic_slice_in_dim(vectors, m * width, width, 1)
    mixed_here = mixed
    mixed_there = lax.ppermute(mixed, ("dp", "mp"), crossing)

    d_normed, d_normed_sent = scatter_group(d_terms, (), (both_term, d_terms[0], mixed_here, pair_ready))
    gain_here = small_of(v, 0)
    x_hat = x_own.astype(F32) * scale_in
    grad_norm_in = jnp.sum(d_normed * x_hat, 0)
    d_x_hat = d_normed * gain_here
    in_dot = sum_group(jnp.sum(d_x_hat * x_hat, 1))[:, None] / full
    d_resid_here = join(
        [cols_of(value, v, width) for value in d_resids],
        lambda k: q ^ k,
        chunk,
        (rows, width),
        0,
        BF16,
    )
    d_tokens = d_resid_here.astype(F32) + scale_in * (d_x_hat - x_hat * in_dot)
    d_tokens_there = lax.ppermute(d_tokens.astype(BF16), ("dp", "mp"), crossing)

    mixed = jnp.where(c == part, mixed_here, after(mixed_there, d_normed))

    def gates_of(*gates):
        return (gates[0],) * (seq_bits - 1) + (gates[1],)

    out_sum = sync(after(out_term, later_in), straight, gates_of(d_terms[0], forget_term))
    go_sum = sync(after(gate_out_term, later_in), crossed, gates_of(d_terms[0], forget_term))
    in_sum = sync(in_term, straight, gates_of(d_terms[0], d_normed))
    forget_sum = sync(forget_term, crossed, gates_of(d_terms[0], d_normed))
    grad_down = spread(down_ready)
    grad_pair = spread(pair_ready)
    mix_sum = jnp.concatenate((in_sum, forget_sum, go_sum), 1)
    mix_ready = combine(after(mix_sum, pair_ready), in_dot, in_dot)
    out_ready = combine(after(out_sum, pair_ready), in_dot, in_dot)
    grad_mix = spread(mix_ready)
    grad_out = spread(out_ready)

    for bit in bits_of(n_seq):
        there = lax.ppermute(grad_norm_in, "seq", [(i, i ^ bit) for i in range(n_seq)])
        grad_norm_in = grad_norm_in + there
    other_half = lax.ppermute(grad_norm_in, "mp", [(i, i ^ half) for i in range(n_mp)])
    grad_norm_in = grad_norm_in + other_half
    other_core = lax.ppermute(grad_norm_in, "dp", [(0, 1), (1, 0)])
    grad_norm_in = jnp.where(c == part, grad_norm_in, other_core)

    d_tokens = jnp.where(c == part, d_tokens, d_tokens_there.astype(F32))

    return (
        mixed.reshape(seqs, length, width),
        d_tokens.reshape(seqs, length, width),
        grad_norm_in,
        grad_mix[:, :width].astype(F32),
        grad_mix[:, width : 2 * width].astype(F32),
        grad_mix[:, 2 * width :].astype(F32),
        vectors[0],
        grad_out.astype(F32),
        vectors[1],
        grad_pair[:, :ff].astype(F32),
        grad_pair[:, ff:].astype(F32),
        grad_down.astype(F32),
    )


def solution(mesh):
    acts = P("dp", "seq", "mp")
    cols, rows, vec = (P(None, "mp"), P("mp", None), P("mp"))
    in_specs = (acts, acts, P("dp"), P(), vec, vec, cols, cols, cols, vec, rows, vec, cols, cols, rows)
    out_specs = (acts, acts, vec, cols, cols, cols, vec, rows, vec, cols, cols, rows)
    return jax.shard_map(
        per_device, mesh=mesh, in_specs=in_specs, out_specs=out_specs, check_vma=False
    )
```
